128 devices in a mesh: row: 8 (over z, y_hi), col: 16 (over x, y_lo, core).
Axes of the slice: x: 4, y: 4 (y_hi: 2, y_lo: 2; y = y_hi * 2 + y_lo), z: 4, core: 2. Of those that a mesh axis runs over, the one named last changes fastest.
Arguments:
- rhs: float32 [4096, 128], P(('row', 'col')), may hold values from -8 to 8
- diag_vals: float32 [4096, 128], P(('row', 'col')), may hold values from 2 to 6
- tiles: float32 [128, 16, 4, 128, 128], P(('row', 'col')), may hold values from -0.1875 to 0.1875
- tile_row: int32 [128, 16, 4], P(('row', 'col')), may hold values from 0 to 31
- tile_col: int32 [128, 16, 4], P(('row', 'col')), may hold values from 0 to 255
Outputs:
- pressure: float32 [4096, 128], P(('row', 'col'))
- residual: float32 [4096, 128], P(('row', 'col'))
The draws below stay inside these ranges and needn't reach their ends.
All inputs are finite; a program needn't handle non-finite values.
Results may differ from the reference program's by a relative error of at most 0.0001.
Values sent between devices are 32-bit elements; how exact they have to be, the bound alone decides.
No kernel may reach another device: no remote copies, remote signals or barrier semaphores. Data moves between devices by JAX's collectives and lax.ppermute only.
A program may use at most 64 MiB of HBM per device.

```python
import jax
import jax.numpy as jnp
from jax import lax

TB = 128
BR_DEV = 32
SLOT = 4
ITERS = 16
NB = 4096
GROUP = 256
N_ROW = 8
N_COL = 16


def place_ends(entries, rng, low, top_value):
    longest = entries.shape.index(max(entries.shape))
    spots = []
    for shift in (0, 1):
        where = [jax.random.randint(jax.random.fold_in(rng, axis), (), 0, length) for axis, length in enumerate(entries.shape)]
        where[longest] = (where[longest] + shift) % entries.shape[longest]
        spots.append(tuple(where))
    return entries.at[spots[0]].set(low).at[spots[1]].set(top_value)


def level_of(own_key, extent, cuts, low, largest):
    def one(dim, blocks):
        draws = jax.random.uniform(jax.random.fold_in(jax.random.fold_in(own_key, 6), dim), (blocks,), jnp.float32, low / len(cuts), largest / len(cuts))
        return jnp.repeat(jnp.exp(draws), extent[dim] // blocks).reshape((-1,) + (1,) * (len(extent) - dim - 1))

    loudness = one(*cuts[0])
    for cut in cuts[1:]:
        loudness = loudness * one(*cut)
    return loudness


def centred(stream_key, extent, spread, bound, cuts=(), kind=jnp.bfloat16):
    level = level_of(stream_key, extent, cuts, -0.22, 0.18) if cuts else 1.0
    result = jax.random.normal(stream_key, extent, jnp.float32) * spread * level
    return jnp.minimum(jnp.maximum(result, -bound), bound).astype(kind)


def setup_inputs(seed: int = 0) -> dict:
    key_list = jax.random.split(jax.random.key(seed), 6)
    return {
        "rhs": centred(key_list[0], (NB, TB), 1.0, 8.0, ((0, 128),), jnp.float32),
        "diag_vals": jnp.clip(2.0 + 4.0 * jax.random.uniform(key_list[1], (NB, TB), jnp.float32) ** level_of(key_list[1], (NB, TB), ((0, 128),), -0.2, 0.2), 2.0, 6.0),
        "tiles": centred(key_list[2], (N_ROW * N_COL, N_COL, SLOT, TB, TB), (4 * TB * N_COL * SLOT // BR_DEV) ** -0.5, 0.1875, ((0, 128),), jnp.float32),
        "tile_row": place_ends(jax.random.randint(key_list[3], (N_ROW * N_COL, N_COL, SLOT), 0, BR_DEV), jax.random.fold_in(key_list[3], 1), 0, BR_DEV - 1).astype(jnp.int32),
        "tile_col": place_ends(jax.random.randint(key_list[4], (N_ROW * N_COL, N_COL, SLOT), 0, GROUP), jax.random.fold_in(key_list[4], 1), 0, GROUP - 1).astype(jnp.int32),
    }


centre = 4.0
half_width = 3.96


def off_part(tiles, row_global, col_global, vec):
    flat = tiles.reshape(-1, TB, TB)
    picked = vec[col_global.reshape(-1)]
    prod = jnp.einsum("tij,tj->ti", flat, picked, precision=lax.Precision.HIGHEST)
    return jax.ops.segment_sum(prod, row_global.reshape(-1), num_segments=NB)


def reference(rhs, diag_vals, tiles, tile_row, tile_col):
    owners = N_ROW * N_COL
    source = jnp.arange(owners, dtype=jnp.int32)[:, None, None]
    group = jnp.arange(N_COL, dtype=jnp.int32)[None, :, None]
    row_global = (source * BR_DEV + tile_row).astype(jnp.int32)
    col_global = (((tile_col // BR_DEV) * N_COL + group) * BR_DEV + tile_col % BR_DEV).astype(jnp.int32)
    sigma = centre / half_width

    def operate(vec):
        return diag_vals * vec - off_part(tiles, row_global, col_global, vec)

    def advance(index, carry):
        pressure, residual, direction, rho = carry
        pressure = pressure + direction
        residual = residual - operate(direction)
        rho_new = 1.0 / (2.0 * sigma - rho)
        direction = (rho_new * rho) * direction + (2.0 * rho_new / half_width) * residual
        return (pressure, residual, direction, rho_new)

    start = (jnp.zeros_like(rhs), rhs, rhs / centre, jnp.asarray(1.0 / sigma, dtype=jnp.float32))
    pressure, residual, direction, rho = lax.fori_loop(0, ITERS, advance, start)
    return pressure, residual
```

```python
import functools

import jax
import jax.numpy as jnp
import numpy as np
from jax import lax
from jax.experimental import pallas as pl
from jax.experimental.pallas import tpu as pltpu
from jax.sharding import PartitionSpec as P

ITERS = 16

centre = 4.0
half_width = 3.96

BOTH = ("row", "col")
VMEM = pl.BlockSpec(memory_space=pltpu.VMEM)
MIB = 1 << 20


def steps():
    sigma = np.float32(2.0 * (centre / half_width))
    rho = np.float32(1.0 / (centre / half_width))
    pairs = []
    for _ in range(ITERS):
        rho_new = np.float32(1.0) / (sigma - rho)
        pairs.append((float(rho_new * rho), float(np.float32(2.0) * rho_new / np.float32(half_width))))
        rho = rho_new
    return pairs


def three_parts(x):
    high = x.astype(jnp.bfloat16)
    rest = x - high.astype(jnp.float32)
    middle = rest.astype(jnp.bfloat16)
    low = (rest - middle.astype(jnp.float32)).astype(jnp.bfloat16)
    return [high, middle, low]


def to_send(pick, direction):
    parts = three_parts(direction)
    parts.append(jnp.zeros_like(parts[0]))
    return jnp.dot(pick, jnp.concatenate(parts, axis=0), preferred_element_type=jnp.float32)


def tile_kernel(tile_ref, held_ref):
    for pair in range(held_ref.shape[0]):
        for end in range(2):
            flipped = tile_ref[2 * pair + end].T
            high = flipped.astype(jnp.bfloat16)
            low = (flipped - high.astype(jnp.float32)).astype(jnp.bfloat16)
            order = flipped.shape[0]
            held_ref[pair, :order, end * order : (end + 1) * order] = high
            held_ref[pair, order:, end * order : (end + 1) * order] = low


def start_kernel(want_ref, mine_ref, rhs_ref, pick_ref, send_ref, direction_ref):
    pick = jnp.where(want_ref[...] == mine_ref[...], 1.0, 0.0).astype(jnp.bfloat16)
    pick_ref[...] = pick
    direction = rhs_ref[...] * (1.0 / centre)
    direction_ref[...] = direction
    send_ref[...] = to_send(pick, direction)


def step_kernel(keep, gain, last, got_ref, held_ref, place_ref, pick_ref, diag_ref, pressure_ref, residual_ref, direction_ref, *out_refs):
    senders, wanted, order = got_ref.shape
    vec = got_ref[0]
    for sender in range(1, senders):
        vec = vec + got_ref[sender]
    high = vec.astype(jnp.bfloat16).astype(jnp.float32)
    low = vec - high
    lane_row = lax.broadcasted_iota(jnp.int32, (8, order), 0)
    products = []
    for block in range(wanted // 8):
        rows = slice(8 * block, 8 * block + 8)
        left = jnp.concatenate([high[rows], low[rows]], axis=0).astype(jnp.bfloat16)
        left = jnp.concatenate([left, left], axis=1)
        total = jnp.zeros((8, order), jnp.float32)
        for pair in range(4):
            out = jnp.dot(left, held_ref[4 * block + pair], preferred_element_type=jnp.float32)
            both = out[:8] + out[8:]
            for end in range(2):
                total = jnp.where(lane_row == 2 * pair + end, both[:, end * order : (end + 1) * order], total)
        products.append(total)
    products = jnp.concatenate(products, axis=0)
    off = jnp.dot(place_ref[...], jnp.concatenate(three_parts(products), axis=0), preferred_element_type=jnp.float32)
    direction = direction_ref[...]
    residual = residual_ref[...] - (diag_ref[...] * direction - off)
    out_refs[0][...] = pressure_ref[...] + direction
    out_refs[1][...] = residual
    if not last:
        direction = keep * direction + gain * residual
        out_refs[2][...] = direction
        out_refs[3][...] = to_send(pick_ref[...], direction)


def per_device(rhs, diag_vals, tiles, tile_row, tile_col):
    owned, order = rhs.shape
    _, groups, slots = tile_col.shape
    devices = lax.axis_size(BOTH)
    senders = devices // groups
    wanted = groups * slots
    f32 = jnp.float32

    asked = jnp.broadcast_to(tile_col[0][None, :, :, None], (senders, groups, slots, order)).reshape(devices, slots, order)
    want = lax.all_to_all(asked, BOTH, 0, 0, tiled=True).reshape(devices * slots, order)

    held = pl.pallas_call(
        tile_kernel,
        grid=(8,),
        in_specs=[pl.BlockSpec((wanted // 8, order, order), lambda i: (i, 0, 0))],
        out_specs=pl.BlockSpec((wanted // 16, 2 * order, 2 * order), lambda i: (i, 0, 0)),
        out_shape=jax.ShapeDtypeStruct((wanted // 2, 2 * order, 2 * order), jnp.bfloat16),
        compiler_params=pltpu.CompilerParams(vmem_limit_bytes=8 * MIB),
    )(tiles.reshape(wanted, order, order))

    targets = jnp.tile(tile_row.reshape(wanted), 3)
    place = (jnp.arange(owned, dtype=jnp.int32)[:, None] == targets[None, :]).astype(jnp.bfloat16)

    lane = jnp.arange(order, dtype=jnp.int32)
    mine = jnp.where(lane < 3 * owned, lax.axis_index("row") * owned + lane % owned, -1)[None, :]
    pick, send, direction = pl.pallas_call(
        start_kernel,
        in_specs=[VMEM] * 3,
        out_specs=[VMEM] * 3,
        out_shape=[
            jax.ShapeDtypeStruct((devices * slots, order), jnp.bfloat16),
            jax.ShapeDtypeStruct((devices * slots, order), f32),
            jax.ShapeDtypeStruct((owned, order), f32),
        ],
        compiler_params=pltpu.CompilerParams(vmem_limit_bytes=8 * MIB),
    )(want, mine, rhs)

    small = jax.ShapeDtypeStruct((owned, order), f32)
    pressure, residual = jnp.zeros_like(rhs), rhs
    for index, (keep, gain) in enumerate(steps()):
        last = index == ITERS - 1
        got = lax.all_to_all(send.reshape(devices, slots, order), BOTH, 0, 0, tiled=True)
        outs = pl.pallas_call(
            functools.partial(step_kernel, keep, gain, last),
            in_specs=[VMEM] * 8,
            out_specs=[VMEM] * (2 if last else 4),
            out_shape=[small, small] if last else [small, small, small, jax.ShapeDtypeStruct((devices * slots, order), f32)],
            compiler_params=pltpu.CompilerParams(vmem_limit_bytes=16 * MIB),
        )(got.reshape(senders, wanted, order), held, place, pick, diag_vals, pressure, residual, direction)
        pressure, residual = outs[:2]
        if not last:
            direction, send = outs[2:]
    return (pressure, residual)


def solution(mesh):
    return jax.shard_map(
        per_device,
        mesh=mesh,
        in_specs=(
            P(("row", "col"), None),
            P(("row", "col"), None),
            P(("row", "col"), None, None, None, None),
            P(("row", "col"), None, None),
            P(("row", "col"), None, None),
        ),
        out_specs=(P(("row", "col"), None), P(("row", "col"), None)),
        check_vma=False,
    )
```

```python
import functools

import jax
import jax.numpy as jnp
import numpy as np
from jax import lax
from jax.experimental import pallas as pl
from jax.experimental.pallas import tpu as pltpu
from jax.sharding import PartitionSpec as P

ITERS = 16

centre = 4.0
half_width = 3.96

BOTH = ("row", "col")
VMEM = pl.BlockSpec(memory_space=pltpu.VMEM)
MIB = 1 << 20


def steps():
    sigma = np.float32(2.0 * (centre / half_width))
    rho = np.float32(1.0 / (centre / half_width))
    pairs = []
    for _ in range(ITERS):
        rho_new = np.float32(1.0) / (sigma - rho)
        pairs.append((float(rho_new * rho), float(np.float32(2.0) * rho_new / np.float32(half_width))))
        rho = rho_new
    return pairs


def three_parts(x):
    high = x.astype(jnp.bfloat16)
    rest = x - high.astype(jnp.float32)
    middle = rest.astype(jnp.bfloat16)
    low = (rest - middle.astype(jnp.float32)).astype(jnp.bfloat16)
    return [high, middle, low]


def to_send(pick, direction):
    parts = three_parts(direction)
    parts.append(jnp.zeros_like(parts[0]))
    return jnp.dot(pick, jnp.concatenate(parts, axis=0), preferred_element_type=jnp.float32)


def ask_kernel(col_ref, ask_ref):
    slots, groups = col_ref.shape
    devices, lanes = ask_ref.shape
    wide = jnp.concatenate([col_ref[...], jnp.zeros((slots, lanes - groups), jnp.int32)], axis=1)
    wide = jnp.concatenate([wide, jnp.zeros((lanes - slots, lanes), jnp.int32)], axis=0)
    rows = wide.T[:groups]
    for first in range(0, devices, groups):
        ask_ref[first : first + groups] = rows


def tile_kernel(tile_ref, place_ref, mine_ref, held_ref):
    for tile in range(held_ref.shape[0]):
        flipped = tile_ref[tile].T
        order = flipped.shape[0]
        high = flipped.astype(jnp.bfloat16)
        held_ref[tile, :order] = high
        held_ref[tile, order:] = (flipped - high.astype(jnp.float32)).astype(jnp.bfloat16)


def begin_kernel(rhs_ref, held_ref, direction_ref):
    direction_ref[...] = rhs_ref[...] * (1.0 / centre)


def start_kernel(want_ref, mine_ref, direction_ref, pick_ref, send_ref, spread_ref):
    devices, lanes = want_ref.shape
    slots = spread_ref.shape[0] // devices
    mine = mine_ref[...]
    for slot in range(slots):
        asked = jnp.broadcast_to(want_ref[:, slot : slot + 1], (devices, lanes))
        spread_ref[pl.ds(slot, devices, stride=slots), :] = jnp.where(asked == mine, 1.0, 0.0)
    pick = spread_ref[...].astype(jnp.bfloat16)
    pick_ref[...] = pick
    send_ref[...] = to_send(pick, direction_ref[...])


def step_kernel(keep, gain, first, last, *refs):
    got_ref, held_ref, place_ref, pick_ref, diag_ref, direction_ref, residual_ref = refs[:7]
    out_refs = refs[7:] if first else refs[8:]
    senders, wanted, order = got_ref.shape
    vec = got_ref[0]
    for sender in range(1, senders):
        vec = vec + got_ref[sender]
    high = vec.astype(jnp.bfloat16).astype(jnp.float32)
    low = vec - high
    lane_row = lax.broadcasted_iota(jnp.int32, (8, order), 0)
    products = []
    for block in range(wanted // 8):
        rows = slice(8 * block, 8 * block + 8)
        left = jnp.concatenate([high[rows], low[rows]], axis=0).astype(jnp.bfloat16)
        left = jnp.concatenate([left, left], axis=1)
        total = jnp.zeros((8, order), jnp.float32)
        for slot in range(8):
            out = jnp.dot(left, held_ref[8 * block + slot], preferred_element_type=jnp.float32)
            total = jnp.where(lane_row == slot, out[:8] + out[8:], total)
        products.append(total)
    products = jnp.concatenate(products, axis=0)
    off = jnp.dot(place_ref[...], jnp.concatenate(three_parts(products), axis=0), preferred_element_type=jnp.float32)
    direction = direction_ref[...]
    residual = residual_ref[...] - (diag_ref[...] * direction - off)
    out_refs[0][...] = direction if first else refs[7][...] + direction
    out_refs[1][...] = residual
    if not last:
        direction = keep * direction + gain * residual
        out_refs[2][...] = direction
        out_refs[3][...] = to_send(pick_ref[...], direction)


def per_device(rhs, diag_vals, tiles, tile_row, tile_col):
    owned, order = rhs.shape
    _, groups, slots = tile_col.shape
    devices = lax.axis_size(BOTH)
    senders = devices // groups
    wanted = groups * slots
    f32 = jnp.float32

    asked = pl.pallas_call(
        ask_kernel,
        in_specs=[VMEM],
        out_specs=VMEM,
        out_shape=jax.ShapeDtypeStruct((devices, order), jnp.int32),
        compiler_params=pltpu.CompilerParams(vmem_limit_bytes=4 * MIB),
    )(tile_col[0].T)
    want = lax.all_to_all(asked[:, None], BOTH, 0, 0, tiled=True)[:, 0]

    targets = jnp.tile(tile_row.reshape(wanted), 3)
    place = (jnp.arange(owned, dtype=jnp.int32)[:, None] == targets[None, :]).astype(jnp.bfloat16)
    lane = jnp.arange(order, dtype=jnp.int32)
    mine = jnp.where(lane < 3 * owned, lax.axis_index("row") * owned + lane % owned, -1)[None, :]

    chunk = wanted // 8
    held = pl.pallas_call(
        tile_kernel,
        grid=(8,),
        in_specs=[
            pl.BlockSpec((chunk, order, order), lambda i: (i, 0, 0)),
            pl.BlockSpec(place.shape, lambda i: (0, 0)),
            pl.BlockSpec(mine.shape, lambda i: (0, 0)),
        ],
        out_specs=pl.BlockSpec((chunk, 2 * order, order), lambda i: (i, 0, 0)),
        out_shape=jax.ShapeDtypeStruct((wanted, 2 * order, order), jnp.bfloat16),
        compiler_params=pltpu.CompilerParams(vmem_limit_bytes=8 * MIB),
    )(tiles.reshape(wanted, order, order), place, mine)

    small = jax.ShapeDtypeStruct((owned, order), f32)
    direction = pl.pallas_call(
        begin_kernel,
        in_specs=[VMEM] * 2,
        out_specs=VMEM,
        out_shape=small,
        compiler_params=pltpu.CompilerParams(vmem_limit_bytes=8 * MIB),
    )(rhs, held)

    pick, send = pl.pallas_call(
        start_kernel,
        in_specs=[VMEM] * 3,
        out_specs=[VMEM] * 2,
        out_shape=[
            jax.ShapeDtypeStruct((devices * slots, order), jnp.bfloat16),
            jax.ShapeDtypeStruct((devices * slots, order), f32),
        ],
        scratch_shapes=[pltpu.VMEM((devices * slots, order), f32)],
        cost_estimate=pl.CostEstimate(flops=10**10, transcendentals=0, bytes_accessed=4 * 10**7),
        compiler_params=pltpu.CompilerParams(vmem_limit_bytes=16 * MIB),
    )(want, mine, direction)

    pressure, residual = [], rhs
    for index, (keep, gain) in enumerate(steps()):
        first, last = index == 0, index == ITERS - 1
        got = lax.all_to_all(send.reshape(devices, slots, order), BOTH, 0, 0, tiled=True)
        outs = pl.pallas_call(
            functools.partial(step_kernel, keep, gain, first, last),
            in_specs=[VMEM] * (7 if first else 8),
            out_specs=[VMEM] * (2 if last else 4),
            out_shape=[small, small] if last else [small, small, small, jax.ShapeDtypeStruct((devices * slots, order), f32)],
            compiler_params=pltpu.CompilerParams(vmem_limit_bytes=16 * MIB),
        )(got.reshape(senders, wanted, order), held, place, pick, diag_vals, direction, residual, *pressure)
        pressure, residual = [outs[0]], outs[1]
        if not last:
            direction, send = outs[2:]
    return (pressure[0], residual)


def solution(mesh):
    return jax.shard_map(
        per_device,
        mesh=mesh,
        in_specs=(
            P(("row", "col"), None),
            P(("row", "col"), None),
            P(("row", "col"), None, None, None, None),
            P(("row", "col"), None, None),
            P(("row", "col"), None, None),
        ),
        out_specs=(P(("row", "col"), None), P(("row", "col"), None)),
        check_vma=False,
    )
```

```python
import functools

import jax
import jax.numpy as jnp
import numpy as np
from jax import lax
from jax.experimental import pallas as pl
from jax.experimental.pallas import tpu as pltpu
from jax.sharding import PartitionSpec as P

ITERS = 16

centre = 4.0
half_width = 3.96

BOTH = ("row", "col")
VMEM = pl.BlockSpec(memory_space=pltpu.VMEM)
MIB = 1 << 20


def steps():
    sigma = np.float32(2.0 * (centre / half_width))
    rho = np.float32(1.0 / (centre / half_width))
    pairs = []
    for _ in range(ITERS):
        rho_new = np.float32(1.0) / (sigma - rho)
        pairs.append((float(rho_new * rho), float(np.float32(2.0) * rho_new / np.float32(half_width))))
        rho = rho_new
    return pairs


def three_parts(x):
    high = x.astype(jnp.bfloat16)
    rest = x - high.astype(jnp.float32)
    middle = rest.astype(jnp.bfloat16)
    low = (rest - middle.astype(jnp.float32)).astype(jnp.bfloat16)
    return [high, middle, low]


def to_send(pick, direction):
    parts = three_parts(direction)
    parts.append(jnp.zeros_like(parts[0]))
    return jnp.dot(pick, jnp.concatenate(parts, axis=0), preferred_element_type=jnp.float32)


def ask_kernel(col_ref, ask_ref):
    slots, groups = col_ref.shape
    devices, lanes = ask_ref.shape
    wide = jnp.concatenate([col_ref[...], jnp.zeros((slots, lanes - groups), jnp.int32)], axis=1)
    wide = jnp.concatenate([wide, jnp.zeros((lanes - slots, lanes), jnp.int32)], axis=0)
    rows = wide.T[:groups]
    for first in range(0, devices, groups):
        ask_ref[first : first + groups] = rows


def tile_kernel(tile_hbm, row_ref, rhs_ref, mine_ref, held_hbm, place_ref, direction_ref, tile_buf, held_buf, in_sem, out_sem):
    chunks = in_sem.shape[0]
    size = tile_hbm.shape[0] // chunks
    order = tile_hbm.shape[-1]
    fetches = [pltpu.make_async_copy(tile_hbm.at[pl.ds(c * size, size)], tile_buf.at[pl.ds(c * size, size)], in_sem.at[c]) for c in range(chunks)]
    stores = [pltpu.make_async_copy(held_buf.at[pl.ds(c * size, size)], held_hbm.at[pl.ds(c * size, size)], out_sem.at[c]) for c in range(chunks)]
    for fetch in fetches:
        fetch.start()
    direction_ref[...] = rhs_ref[...] * (1.0 / centre)
    slots, groups = row_ref.shape
    owned, spread = place_ref.shape
    wanted = slots * groups
    source = lax.broadcasted_iota(jnp.int32, (groups, spread), 0)
    target = lax.broadcasted_iota(jnp.int32, (groups, spread), 1) % wanted
    targets = jnp.zeros((8, spread), jnp.float32)
    rows = row_ref[...].astype(jnp.float32)
    for slot in range(slots):
        expand = jnp.where(target == source * slots + slot, 1.0, 0.0).astype(jnp.bfloat16)
        line = jnp.broadcast_to(rows[slot : slot + 1], (8, groups)).astype(jnp.bfloat16)
        targets = targets + jnp.dot(line, expand, preferred_element_type=jnp.float32)
    block = lax.broadcasted_iota(jnp.int32, (owned, spread), 0)
    place_ref[...] = jnp.where(block == targets[:1].astype(jnp.int32), 1.0, 0.0).astype(jnp.bfloat16)
    for c in range(chunks):
        fetches[c].wait()
        for tile in range(c * size, (c + 1) * size):
            flipped = tile_buf[tile].T
            high = flipped.astype(jnp.bfloat16)
            held_buf[tile, :order] = high
            held_buf[tile, order:] = (flipped - high.astype(jnp.float32)).astype(jnp.bfloat16)
        stores[c].start()
    for store in stores:
        store.wait()


def start_kernel(want_ref, mine_ref, direction_ref, pick_ref, send_ref, spread_ref):
    devices, lanes = want_ref.shape
    slots = spread_ref.shape[0] // devices
    mine = mine_ref[...]
    for slot in range(slots):
        asked = jnp.broadcast_to(want_ref[:, slot : slot + 1], (devices, lanes))
        spread_ref[pl.ds(slot, devices, stride=slots), :] = jnp.where(asked == mine, 1.0, 0.0)
    pick = spread_ref[...].astype(jnp.bfloat16)
    pick_ref[...] = pick
    send_ref[...] = to_send(pick, direction_ref[...])


def step_kernel(keep, gain, first, last, *refs):
    got_ref, held_ref, place_ref, pick_ref, diag_ref, direction_ref, residual_ref = refs[:7]
    out_refs = refs[7:] if first else refs[8:]
    senders, wanted, order = got_ref.shape
    vec = got_ref[0]
    for sender in range(1, senders):
        vec = vec + got_ref[sender]
    high = vec.astype(jnp.bfloat16).astype(jnp.float32)
    low = vec - high
    lane_row = lax.broadcasted_iota(jnp.int32, (8, order), 0)
    products = []
    for block in range(wanted // 8):
        rows = slice(8 * block, 8 * block + 8)
        left = jnp.concatenate([high[rows], low[rows]], axis=0).astype(jnp.bfloat16)
        left = jnp.concatenate([left, left], axis=1)
        total = jnp.zeros((8, order), jnp.float32)
        for slot in range(8):
            out = jnp.dot(left, held_ref[8 * block + slot], preferred_element_type=jnp.float32)
            total = jnp.where(lane_row == slot, out[:8] + out[8:], total)
        products.append(total)
    products = jnp.concatenate(products, axis=0)
    off = jnp.dot(place_ref[...], jnp.concatenate(three_parts(products), axis=0), preferred_element_type=jnp.float32)
    direction = direction_ref[...]
    residual = residual_ref[...] - (diag_ref[...] * direction - off)
    out_refs[0][...] = direction if first else refs[7][...] + direction
    out_refs[1][...] = residual
    if not last:
        direction = keep * direction + gain * residual
        out_refs[2][...] = direction
        out_refs[3][...] = to_send(pick_ref[...], direction)


def per_device(rhs, diag_vals, tiles, tile_row, tile_col):
    owned, order = rhs.shape
    _, groups, slots = tile_col.shape
    devices = lax.axis_size(BOTH)
    senders = devices // groups
    wanted = groups * slots
    f32 = jnp.float32

    asked = pl.pallas_call(
        ask_kernel,
        in_specs=[VMEM],
        out_specs=VMEM,
        out_shape=jax.ShapeDtypeStruct((devices, order), jnp.int32),
        compiler_params=pltpu.CompilerParams(vmem_limit_bytes=4 * MIB),
    )(tile_col[0].T)
    want = lax.all_to_all(asked[:, None], BOTH, 0, 0, tiled=True)[:, 0]

    lane = jnp.arange(order, dtype=jnp.int32)
    mine = jnp.where(lane < 3 * owned, lax.axis_index("row") * owned + lane % owned, -1)[None, :]

    chunks = 8
    small = jax.ShapeDtypeStruct((owned, order), f32)
    held, place, direction = pl.pallas_call(
        tile_kernel,
        in_specs=[pl.BlockSpec(memory_space=pltpu.HBM), VMEM, VMEM, VMEM],
        out_specs=[pl.BlockSpec(memory_space=pltpu.HBM), VMEM, VMEM],
        out_shape=[
            pltpu.HBM((wanted, 2 * order, order), jnp.bfloat16),
            jax.ShapeDtypeStruct((owned, 3 * wanted), jnp.bfloat16),
            small,
        ],
        scratch_shapes=[
            pltpu.VMEM((wanted, order, order), f32),
            pltpu.VMEM((wanted, 2 * order, order), jnp.bfloat16),
            pltpu.SemaphoreType.DMA((chunks,)),
            pltpu.SemaphoreType.DMA((chunks,)),
        ],
        compiler_params=pltpu.CompilerParams(vmem_limit_bytes=16 * MIB),
    )(pltpu.with_memory_space_constraint(tiles.reshape(wanted, order, order), pltpu.HBM), tile_row[0].T, rhs, mine)

    pick, send = pl.pallas_call(
        start_kernel,
        in_specs=[VMEM] * 3,
        out_specs=[VMEM] * 2,
        out_shape=[
            jax.ShapeDtypeStruct((devices * slots, order), jnp.bfloat16),
            jax.ShapeDtypeStruct((devices * slots, order), f32),
        ],
        scratch_shapes=[pltpu.VMEM((devices * slots, order), f32)],
        cost_estimate=pl.CostEstimate(flops=10**10, transcendentals=0, bytes_accessed=4 * 10**7),
        compiler_params=pltpu.CompilerParams(vmem_limit_bytes=16 * MIB),
    )(want, mine, direction)

    pressure, residual = [], rhs
    for index, (keep, gain) in enumerate(steps()):
        first, last = index == 0, index == ITERS - 1
        got = lax.all_to_all(send.reshape(devices, slots, order), BOTH, 0, 0, tiled=True)
        outs = pl.pallas_call(
            functools.partial(step_kernel, keep, gain, first, last),
            in_specs=[VMEM] * (7 if first else 8),
            out_specs=[VMEM] * (2 if last else 4),
            out_shape=[small, small] if last else [small, small, small, jax.ShapeDtypeStruct((devices * slots, order), f32)],
            compiler_params=pltpu.CompilerParams(vmem_limit_bytes=16 * MIB),
        )(got.reshape(senders, wanted, order), held, place, pick, diag_vals, direction, residual, *pressure)
        pressure, residual = [outs[0]], outs[1]
        if not last:
            direction, send = outs[2:]
    return (pressure[0], residual)


def solution(mesh):
    return jax.shard_map(
        per_device,
        mesh=mesh,
        in_specs=(
            P(("row", "col"), None),
            P(("row", "col"), None),
            P(("row", "col"), None, None, None, None),
            P(("row", "col"), None, None),
            P(("row", "col"), None, None),
        ),
        out_specs=(P(("row", "col"), None), P(("row", "col"), None)),
        check_vma=False,
    )
```

```python
import functools

import jax
import jax.numpy as jnp
import numpy as np
from jax import lax
from jax.experimental import pallas as pl
from jax.experimental.pallas import tpu as pltpu
from jax.sharding import PartitionSpec as P

ITERS = 16

centre = 4.0
half_width = 3.96

BOTH = ("row", "col")
VMEM = pl.BlockSpec(memory_space=pltpu.VMEM)
MIB = 1 << 20


def in_hbm(x):
    return pltpu.with_memory_space_constraint(x, pltpu.HBM)


def steps():
    sigma = np.float32(2.0 * (centre / half_width))
    rho = np.float32(1.0 / (centre / half_width))
    pairs = []
    for _ in range(ITERS):
        rho_new = np.float32(1.0) / (sigma - rho)
        pairs.append((float(rho_new * rho), float(np.float32(2.0) * rho_new / np.float32(half_width))))
        rho = rho_new
    return pairs


def three_parts(x):
    high = x.astype(jnp.bfloat16)
    rest = x - high.astype(jnp.float32)
    middle = rest.astype(jnp.bfloat16)
    low = (rest - middle.astype(jnp.float32)).astype(jnp.bfloat16)
    return [high, middle, low]


def to_send(pick, direction):
    parts = three_parts(direction)
    parts.append(jnp.zeros_like(parts[0]))
    return jnp.dot(pick, jnp.concatenate(parts, axis=0), preferred_element_type=jnp.float32)


def ask_kernel(col_ref, ask_ref):
    slots, groups = col_ref.shape
    devices, lanes = ask_ref.shape
    wide = jnp.concatenate([col_ref[...], jnp.zeros((slots, lanes - groups), jnp.int32)], axis=1)
    wide = jnp.concatenate([wide, jnp.zeros((lanes - slots, lanes), jnp.int32)], axis=0)
    rows = wide.T[:groups]
    for first in range(0, devices, groups):
        ask_ref[first : first + groups] = rows


def tile_kernel(tile_hbm, row_hbm, rhs_hbm, mine_ref, held_hbm, place_ref, direction_ref, tile_buf, held_buf, row_ref, rhs_ref, in_sem, out_sem, row_sem, rhs_sem):
    chunks = in_sem.shape[0]
    size = tile_hbm.shape[0] // chunks
    order = tile_hbm.shape[-1]
    fetches = [pltpu.make_async_copy(tile_hbm.at[pl.ds(c * size, size)], tile_buf.at[pl.ds(c * size, size)], in_sem.at[c]) for c in range(chunks)]
    stores = [pltpu.make_async_copy(held_buf.at[pl.ds(c * size, size)], held_hbm.at[pl.ds(c * size, size)], out_sem.at[c]) for c in range(chunks)]
    small = [pltpu.make_async_copy(row_hbm, row_ref, row_sem), pltpu.make_async_copy(rhs_hbm, rhs_ref, rhs_sem)]
    for fetch in small + fetches:
        fetch.start()
    for fetch in small:
        fetch.wait()
    direction_ref[...] = rhs_ref[...] * (1.0 / centre)
    slots, groups = row_ref.shape
    owned, spread = place_ref.shape
    wanted = slots * groups
    source = lax.broadcasted_iota(jnp.int32, (groups, spread), 0)
    target = lax.broadcasted_iota(jnp.int32, (groups, spread), 1) % wanted
    targets = jnp.zeros((8, spread), jnp.float32)
    rows = row_ref[...].astype(jnp.float32)
    for slot in range(slots):
        expand = jnp.where(target == source * slots + slot, 1.0, 0.0).astype(jnp.bfloat16)
        line = jnp.broadcast_to(rows[slot : slot + 1], (8, groups)).astype(jnp.bfloat16)
        targets = targets + jnp.dot(line, expand, preferred_element_type=jnp.float32)
    block = lax.broadcasted_iota(jnp.int32, (owned, spread), 0)
    place_ref[...] = jnp.where(block == targets[:1].astype(jnp.int32), 1.0, 0.0).astype(jnp.bfloat16)
    for c in range(chunks):
        fetches[c].wait()
        for tile in range(c * size, (c + 1) * size):
            flipped = tile_buf[tile].T
            high = flipped.astype(jnp.bfloat16)
            held_buf[tile, :order] = high
            held_buf[tile, order:] = (flipped - high.astype(jnp.float32)).astype(jnp.bfloat16)
        stores[c].start()
    for store in stores:
        store.wait()


def start_kernel(want_ref, mine_ref, direction_ref, pick_ref, send_ref, spread_ref):
    devices, lanes = want_ref.shape
    slots = spread_ref.shape[0] // devices
    mine = mine_ref[...]
    for slot in range(slots):
        asked = jnp.broadcast_to(want_ref[:, slot : slot + 1], (devices, lanes))
        spread_ref[pl.ds(slot, devices, stride=slots), :] = jnp.where(asked == mine, 1.0, 0.0)
    pick = spread_ref[...].astype(jnp.bfloat16)
    pick_ref[...] = pick
    send_ref[...] = to_send(pick, direction_ref[...])


def step_kernel(keep, gain, first, last, *refs):
    got_ref, held_ref, place_ref, pick_ref, diag_ref, direction_ref, residual_ref = refs[:7]
    out_refs = refs[7:] if first else refs[8:]
    senders, wanted, order = got_ref.shape
    vec = got_ref[0]
    for sender in range(1, senders):
        vec = vec + got_ref[sender]
    high = vec.astype(jnp.bfloat16).astype(jnp.float32)
    low = vec - high
    lane_row = lax.broadcasted_iota(jnp.int32, (8, order), 0)
    products = []
    for block in range(wanted // 8):
        rows = slice(8 * block, 8 * block + 8)
        left = jnp.concatenate([high[rows], low[rows]], axis=0).astype(jnp.bfloat16)
        left = jnp.concatenate([left, left], axis=1)
        total = jnp.zeros((8, order), jnp.float32)
        for slot in range(8):
            out = jnp.dot(left, held_ref[8 * block + slot], preferred_element_type=jnp.float32)
            total = jnp.where(lane_row == slot, out[:8] + out[8:], total)
        products.append(total)
    products = jnp.concatenate(products, axis=0)
    off = jnp.dot(place_ref[...], jnp.concatenate(three_parts(products), axis=0), preferred_element_type=jnp.float32)
    direction = direction_ref[...]
    residual = residual_ref[...] - (diag_ref[...] * direction - off)
    out_refs[0][...] = direction if first else refs[7][...] + direction
    out_refs[1][...] = residual
    if not last:
        direction = keep * direction + gain * residual
        out_refs[2][...] = direction
        out_refs[3][...] = to_send(pick_ref[...], direction)


def per_device(rhs, diag_vals, tiles, tile_row, tile_col):
    owned, order = rhs.shape
    _, groups, slots = tile_col.shape
    devices = lax.axis_size(BOTH)
    senders = devices // groups
    wanted = groups * slots
    f32 = jnp.float32

    asked = pl.pallas_call(
        ask_kernel,
        in_specs=[VMEM],
        out_specs=VMEM,
        out_shape=jax.ShapeDtypeStruct((devices, order), jnp.int32),
        compiler_params=pltpu.CompilerParams(vmem_limit_bytes=4 * MIB),
    )(tile_col[0].T)
    want = lax.all_to_all(asked[:, None], BOTH, 0, 0, tiled=True)[:, 0]

    lane = jnp.arange(order, dtype=jnp.int32)
    mine = jnp.where(lane < 3 * owned, lax.axis_index("row") * owned + lane % owned, -1)[None, :]

    chunks = 8
    small = jax.ShapeDtypeStruct((owned, order), f32)
    held, place, direction = pl.pallas_call(
        tile_kernel,
        in_specs=[pl.BlockSpec(memory_space=pltpu.HBM)] * 3 + [VMEM],
        out_specs=[pl.BlockSpec(memory_space=pltpu.HBM), VMEM, VMEM],
        out_shape=[
            pltpu.HBM((wanted, 2 * order, order), jnp.bfloat16),
            jax.ShapeDtypeStruct((owned, 3 * wanted), jnp.bfloat16),
            small,
        ],
        scratch_shapes=[
            pltpu.VMEM((wanted, order, order), f32),
            pltpu.VMEM((wanted, 2 * order, order), jnp.bfloat16),
            pltpu.VMEM((slots, groups), jnp.int32),
            pltpu.VMEM((owned, order), f32),
            pltpu.SemaphoreType.DMA((chunks,)),
            pltpu.SemaphoreType.DMA((chunks,)),
            pltpu.SemaphoreType.DMA,
            pltpu.SemaphoreType.DMA,
        ],
        compiler_params=pltpu.CompilerParams(vmem_limit_bytes=16 * MIB),
    )(in_hbm(tiles.reshape(wanted, order, order)), in_hbm(tile_row[0].T), in_hbm(rhs), mine)

    pick, send = pl.pallas_call(
        start_kernel,
        in_specs=[VMEM] * 3,
        out_specs=[VMEM] * 2,
        out_shape=[
            jax.ShapeDtypeStruct((devices * slots, order), jnp.bfloat16),
            jax.ShapeDtypeStruct((devices * slots, order), f32),
        ],
        scratch_shapes=[pltpu.VMEM((devices * slots, order), f32)],
        cost_estimate=pl.CostEstimate(flops=10**10, transcendentals=0, bytes_accessed=4 * 10**7),
        compiler_params=pltpu.CompilerParams(vmem_limit_bytes=16 * MIB),
    )(want, mine, direction)

    pressure, residual = [], rhs
    for index, (keep, gain) in enumerate(steps()):
        first, last = index == 0, index == ITERS - 1
        got = lax.all_to_all(send.reshape(devices, slots, order), BOTH, 0, 0, tiled=True)
        outs = pl.pallas_call(
            functools.partial(step_kernel, keep, gain, first, last),
            in_specs=[VMEM] * (7 if first else 8),
            out_specs=[VMEM] * (2 if last else 4),
            out_shape=[small, small] if last else [small, small, small, jax.ShapeDtypeStruct((devices * slots, order), f32)],
            compiler_params=pltpu.CompilerParams(vmem_limit_bytes=16 * MIB),
        )(got.reshape(senders, wanted, order), held, place, pick, diag_vals, direction, residual, *pressure)
        pressure, residual = [outs[0]], outs[1]
        if not last:
            direction, send = outs[2:]
    return (pressure[0], residual)


def solution(mesh):
    return jax.shard_map(
        per_device,
        mesh=mesh,
        in_specs=(
            P(("row", "col"), None),
            P(("row", "col"), None),
            P(("row", "col"), None, None, None, None),
            P(("row", "col"), None, None),
            P(("row", "col"), None, None),
        ),
        out_specs=(P(("row", "col"), None), P(("row", "col"), None)),
        check_vma=False,
    )
```

```python
import functools

import jax
import jax.numpy as jnp
import numpy as np
from jax import lax
from jax.experimental import pallas as pl
from jax.experimental.pallas import tpu as pltpu
from jax.sharding import PartitionSpec as P

ITERS = 16

centre = 4.0
half_width = 3.96

BOTH = ("row", "col")
VMEM = pl.BlockSpec(memory_space=pltpu.VMEM)
MIB = 1 << 20


def in_hbm(x):
    return pltpu.with_memory_space_constraint(x, pltpu.HBM)


def steps():
    sigma = np.float32(2.0 * (centre / half_width))
    rho = np.float32(1.0 / (centre / half_width))
    pairs = []
    for _ in range(ITERS):
        rho_new = np.float32(1.0) / (sigma - rho)
        pairs.append((float(rho_new * rho), float(np.float32(2.0) * rho_new / np.float32(half_width))))
        rho = rho_new
    return pairs


def three_parts(x):
    high = x.astype(jnp.bfloat16)
    rest = x - high.astype(jnp.float32)
    middle = rest.astype(jnp.bfloat16)
    low = (rest - middle.astype(jnp.float32)).astype(jnp.bfloat16)
    return [high, middle, low]


def to_send(pick, direction):
    parts = three_parts(direction)
    parts.append(jnp.zeros_like(parts[0]))
    return jnp.dot(pick, jnp.concatenate(parts, axis=0), preferred_element_type=jnp.float32)


def ask_kernel(col_ref, ask_ref):
    slots, groups = col_ref.shape
    devices, lanes = ask_ref.shape
    wide = jnp.concatenate([col_ref[...], jnp.zeros((slots, lanes - groups), jnp.int32)], axis=1)
    wide = jnp.concatenate([wide, jnp.zeros((lanes - slots, lanes), jnp.int32)], axis=0)
    rows = wide.T[:groups]
    for first in range(0, devices, groups):
        ask_ref[first : first + groups] = rows


def tile_kernel(tile_hbm, row_hbm, rhs_hbm, mine_ref, held_hbm, place_ref, direction_ref, tile_buf, held_buf, row_ref, rhs_ref, in_sem, out_sem, row_sem, rhs_sem):
    chunks = in_sem.shape[0]
    size = tile_hbm.shape[0] // chunks
    order = tile_hbm.shape[-1]
    fetches = [pltpu.make_async_copy(tile_hbm.at[pl.ds(c * size, size)], tile_buf.at[pl.ds(c * size, size)], in_sem.at[c]) for c in range(chunks)]
    stores = [pltpu.make_async_copy(held_buf.at[pl.ds(c * size, size)], held_hbm.at[pl.ds(c * size, size)], out_sem.at[c]) for c in range(chunks)]
    small = [pltpu.make_async_copy(row_hbm, row_ref, row_sem), pltpu.make_async_copy(rhs_hbm, rhs_ref, rhs_sem)]
    for fetch in small + fetches:
        fetch.start()
    for c in range(chunks):
        fetches[c].wait()
        for tile in range(c * size, (c + 1) * size):
            flipped = tile_buf[tile].T
            high = flipped.astype(jnp.bfloat16)
            held_buf[tile, :order] = high
            held_buf[tile, order:] = (flipped - high.astype(jnp.float32)).astype(jnp.bfloat16)
        stores[c].start()
    for fetch in small:
        fetch.wait()
    direction_ref[...] = rhs_ref[...] * (1.0 / centre)
    slots, groups = row_ref.shape
    wanted, owned, spread = place_ref.shape
    source = lax.broadcasted_iota(jnp.int32, (groups, spread), 0)
    target = lax.broadcasted_iota(jnp.int32, (groups, spread), 1)
    targets = jnp.zeros((8, spread), jnp.float32)
    rows = row_ref[...].astype(jnp.float32)
    for slot in range(slots):
        expand = jnp.where(target == source * slots + slot, 1.0, 0.0).astype(jnp.bfloat16)
        line = jnp.broadcast_to(rows[slot : slot + 1], (8, groups)).astype(jnp.bfloat16)
        targets = targets + jnp.dot(line, expand, preferred_element_type=jnp.float32)
    targets = targets.astype(jnp.int32)
    block = lax.broadcasted_iota(jnp.int32, (8, spread), 0)
    for tile in range(wanted):
        line = jnp.broadcast_to(targets[:, tile : tile + 1], (8, spread))
        for first in range(0, owned, 8):
            place_ref[tile, first : first + 8] = jnp.where(block + first == line, 1.0, 0.0)
    for store in stores:
        store.wait()


def start_kernel(want_ref, mine_ref, direction_ref, pick_ref, send_ref, spread_ref):
    devices, lanes = want_ref.shape
    slots = spread_ref.shape[0] // devices
    mine = mine_ref[...]
    for slot in range(slots):
        asked = jnp.broadcast_to(want_ref[:, slot : slot + 1], (devices, lanes))
        spread_ref[pl.ds(slot, devices, stride=slots), :] = jnp.where(asked == mine, 1.0, 0.0)
    pick = spread_ref[...].astype(jnp.bfloat16)
    pick_ref[...] = pick
    send_ref[...] = to_send(pick, direction_ref[...])


def step_kernel(keep, gain, first, last, *refs):
    got_ref, held_ref, place_ref, pick_ref, diag_ref, direction_ref, residual_ref = refs[:7]
    out_refs = refs[7:] if first else refs[8:]
    senders, wanted, order = got_ref.shape
    vec = got_ref[0]
    for sender in range(1, senders):
        vec = vec + got_ref[sender]
    high = vec.astype(jnp.bfloat16).astype(jnp.float32)
    low = vec - high
    off = jnp.zeros(direction_ref.shape, jnp.float32)
    for block in range(wanted // 8):
        rows = slice(8 * block, 8 * block + 8)
        left = jnp.concatenate([high[rows], low[rows]], axis=0).astype(jnp.bfloat16)
        left = jnp.concatenate([left, left], axis=1)
        for slot in range(8):
            out = jnp.dot(left, held_ref[8 * block + slot], preferred_element_type=jnp.float32)
            row = out[slot : slot + 1] + out[8 + slot : 9 + slot]
            off = off + place_ref[8 * block + slot] * row
    direction = direction_ref[...]
    residual = residual_ref[...] - (diag_ref[...] * direction - off)
    out_refs[0][...] = direction if first else refs[7][...] + direction
    out_refs[1][...] = residual
    if not last:
        direction = keep * direction + gain * residual
        out_refs[2][...] = direction
        out_refs[3][...] = to_send(pick_ref[...], direction)


def per_device(rhs, diag_vals, tiles, tile_row, tile_col):
    owned, order = rhs.shape
    _, groups, slots = tile_col.shape
    devices = lax.axis_size(BOTH)
    senders = devices // groups
    wanted = groups * slots
    f32 = jnp.float32

    asked = pl.pallas_call(
        ask_kernel,
        in_specs=[VMEM],
        out_specs=VMEM,
        out_shape=jax.ShapeDtypeStruct((devices, order), jnp.int32),
        compiler_params=pltpu.CompilerParams(vmem_limit_bytes=4 * MIB),
    )(tile_col[0].T)
    want = lax.all_to_all(asked[:, None], BOTH, 0, 0, tiled=True)[:, 0]

    lane = jnp.arange(order, dtype=jnp.int32)
    mine = jnp.where(lane < 3 * owned, lax.axis_index("row") * owned + lane % owned, -1)[None, :]

    chunks = 8
    small = jax.ShapeDtypeStruct((owned, order), f32)
    held, place, direction = pl.pallas_call(
        tile_kernel,
        in_specs=[pl.BlockSpec(memory_space=pltpu.HBM)] * 3 + [VMEM],
        out_specs=[pl.BlockSpec(memory_space=pltpu.HBM), VMEM, VMEM],
        out_shape=[
            pltpu.HBM((wanted, 2 * order, order), jnp.bfloat16),
            jax.ShapeDtypeStruct((wanted, owned, order), f32),
            small,
        ],
        scratch_shapes=[
            pltpu.VMEM((wanted, order, order), f32),
            pltpu.VMEM((wanted, 2 * order, order), jnp.bfloat16),
            pltpu.VMEM((slots, groups), jnp.int32),
            pltpu.VMEM((owned, order), f32),
            pltpu.SemaphoreType.DMA((chunks,)),
            pltpu.SemaphoreType.DMA((chunks,)),
            pltpu.SemaphoreType.DMA,
            pltpu.SemaphoreType.DMA,
        ],
        compiler_params=pltpu.CompilerParams(vmem_limit_bytes=16 * MIB),
    )(in_hbm(tiles.reshape(wanted, order, order)), in_hbm(tile_row[0].T), in_hbm(rhs), mine)

    pick, send = pl.pallas_call(
        start_kernel,
        in_specs=[VMEM] * 3,
        out_specs=[VMEM] * 2,
        out_shape=[
            jax.ShapeDtypeStruct((devices * slots, order), jnp.bfloat16),
            jax.ShapeDtypeStruct((devices * slots, order), f32),
        ],
        scratch_shapes=[pltpu.VMEM((devices * slots, order), f32)],
        cost_estimate=pl.CostEstimate(flops=10**10, transcendentals=0, bytes_accessed=4 * 10**7),
        compiler_params=pltpu.CompilerParams(vmem_limit_bytes=16 * MIB),
    )(want, mine, direction)

    pressure, residual = [], rhs
    for index, (keep, gain) in enumerate(steps()):
        first, last = index == 0, index == ITERS - 1
        got = lax.all_to_all(send.reshape(devices, slots, order), BOTH, 0, 0, tiled=True)
        outs = pl.pallas_call(
            functools.partial(step_kernel, keep, gain, first, last),
            in_specs=[VMEM] * (7 if first else 8),
            out_specs=[VMEM] * (2 if last else 4),
            out_shape=[small, small] if last else [small, small, small, jax.ShapeDtypeStruct((devices * slots, order), f32)],
            compiler_params=pltpu.CompilerParams(vmem_limit_bytes=16 * MIB),
        )(got.reshape(senders, wanted, order), held, place, pick, diag_vals, direction, residual, *pressure)
        pressure, residual = [outs[0]], outs[1]
        if not last:
            direction, send = outs[2:]
    return (pressure[0], residual)


def solution(mesh):
    return jax.shard_map(
        per_device,
        mesh=mesh,
        in_specs=(
            P(("row", "col"), None),
            P(("row", "col"), None),
            P(("row", "col"), None, None, None, None),
            P(("row", "col"), None, None),
            P(("row", "col"), None, None),
        ),
        out_specs=(P(("row", "col"), None), P(("row", "col"), None)),
        check_vma=False,
    )
```

```python
import functools

import jax
import jax.numpy as jnp
import numpy as np
from jax import lax
from jax.experimental import pallas as pl
from jax.experimental.pallas import tpu as pltpu
from jax.sharding import PartitionSpec as P

ITERS = 16

centre = 4.0
half_width = 3.96

BOTH = ("row", "col")
VMEM = pl.BlockSpec(memory_space=pltpu.VMEM)
MIB = 1 << 20


def in_hbm(x):
    return pltpu.with_memory_space_constraint(x, pltpu.HBM)


def steps():
    sigma = np.float32(2.0 * (centre / half_width))
    rho = np.float32(1.0 / (centre / half_width))
    pairs = []
    for _ in range(ITERS):
        rho_new = np.float32(1.0) / (sigma - rho)
        pairs.append((float(rho_new * rho), float(np.float32(2.0) * rho_new / np.float32(half_width))))
        rho = rho_new
    return pairs


def to_send(pick, direction):
    high = direction.astype(jnp.bfloat16)
    low = (direction - high.astype(jnp.float32)).astype(jnp.bfloat16)
    parts = jnp.concatenate([high, low], axis=0)
    return jnp.dot(pick[:, : parts.shape[0]], parts, preferred_element_type=jnp.float32)


def ask_kernel(col_ref, ask_ref):
    slots, groups = col_ref.shape
    devices, lanes = ask_ref.shape
    wide = jnp.concatenate([col_ref[...], jnp.zeros((slots, lanes - groups), jnp.int32)], axis=1)
    wide = jnp.concatenate([wide, jnp.zeros((lanes - slots, lanes), jnp.int32)], axis=0)
    rows = wide.T[:groups]
    for first in range(0, devices, groups):
        ask_ref[first : first + groups] = rows


def tile_kernel(tile_hbm, row_hbm, rhs_hbm, mine_ref, held_hbm, place_ref, direction_ref, tile_buf, held_buf, row_ref, rhs_ref, in_sem, out_sem, row_sem, rhs_sem):
    chunks = in_sem.shape[0]
    size = tile_hbm.shape[0] // chunks
    order = tile_hbm.shape[-1]
    fetches = [pltpu.make_async_copy(tile_hbm.at[pl.ds(c * size, size)], tile_buf.at[pl.ds(c * size, size)], in_sem.at[c]) for c in range(chunks)]
    stores = [pltpu.make_async_copy(held_buf.at[pl.ds(c * size, size)], held_hbm.at[pl.ds(c * size, size)], out_sem.at[c]) for c in range(chunks)]
    small = [pltpu.make_async_copy(row_hbm, row_ref, row_sem), pltpu.make_async_copy(rhs_hbm, rhs_ref, rhs_sem)]
    for fetch in small + fetches:
        fetch.start()
    for c in range(chunks):
        fetches[c].wait()
        for tile in range(c * size, (c + 1) * size):
            flipped = tile_buf[tile].T
            high = flipped.astype(jnp.bfloat16)
            held_buf[tile, :order] = high
            held_buf[tile, order:] = (flipped - high.astype(jnp.float32)).astype(jnp.bfloat16)
        stores[c].start()
    for fetch in small:
        fetch.wait()
    direction_ref[...] = rhs_ref[...] * (1.0 / centre)
    slots, groups = row_ref.shape
    wanted, owned, spread = place_ref.shape
    source = lax.broadcasted_iota(jnp.int32, (groups, spread), 0)
    target = lax.broadcasted_iota(jnp.int32, (groups, spread), 1)
    targets = jnp.zeros((8, spread), jnp.float32)
    rows = row_ref[...].astype(jnp.float32)
    for slot in range(slots):
        expand = jnp.where(target == source * slots + slot, 1.0, 0.0).astype(jnp.bfloat16)
        line = jnp.broadcast_to(rows[slot : slot + 1], (8, groups)).astype(jnp.bfloat16)
        targets = targets + jnp.dot(line, expand, preferred_element_type=jnp.float32)
    targets = targets.astype(jnp.int32)
    block = lax.broadcasted_iota(jnp.int32, (8, spread), 0)
    for tile in range(wanted):
        line = jnp.broadcast_to(targets[:, tile : tile + 1], (8, spread))
        for first in range(0, owned, 8):
            place_ref[tile, first : first + 8] = jnp.where(block + first == line, 1.0, 0.0)
    for store in stores:
        store.wait()


def start_kernel(want_ref, mine_ref, direction_ref, pick_ref, send_ref, spread_ref):
    devices, lanes = want_ref.shape
    slots = spread_ref.shape[0] // devices
    mine = mine_ref[...]
    for slot in range(slots):
        asked = jnp.broadcast_to(want_ref[:, slot : slot + 1], (devices, lanes))
        spread_ref[pl.ds(slot, devices, stride=slots), :] = jnp.where(asked == mine, 1.0, 0.0)
    pick = spread_ref[...].astype(jnp.bfloat16)
    pick_ref[...] = pick
    send_ref[...] = to_send(pick, direction_ref[...])


def step_kernel(keep, gain, first, last, *refs):
    got_ref, held_ref, place_ref, pick_ref, diag_ref, direction_ref, residual_ref = refs[:7]
    out_refs = refs[7:] if first else refs[8:]
    senders, wanted, order = got_ref.shape
    vec = got_ref[0]
    for sender in range(1, senders):
        vec = vec + got_ref[sender]
    high = vec.astype(jnp.bfloat16).astype(jnp.float32)
    low = vec - high
    off = jnp.zeros(direction_ref.shape, jnp.float32)
    for block in range(wanted // 8):
        rows = slice(8 * block, 8 * block + 8)
        left = jnp.concatenate([high[rows], low[rows]], axis=0).astype(jnp.bfloat16)
        left = jnp.concatenate([left, left], axis=1)
        for slot in range(8):
            out = jnp.dot(left, held_ref[8 * block + slot], preferred_element_type=jnp.float32)
            row = out[slot : slot + 1] + out[8 + slot : 9 + slot]
            off = off + place_ref[8 * block + slot] * row
    direction = direction_ref[...]
    residual = residual_ref[...] - (diag_ref[...] * direction - off)
    out_refs[0][...] = direction if first else refs[7][...] + direction
    out_refs[1][...] = residual
    if not last:
        direction = keep * direction + gain * residual
        out_refs[2][...] = direction
        out_refs[3][...] = to_send(pick_ref[...], direction)


def per_device(rhs, diag_vals, tiles, tile_row, tile_col):
    owned, order = rhs.shape
    _, groups, slots = tile_col.shape
    devices = lax.axis_size(BOTH)
    senders = devices // groups
    wanted = groups * slots
    f32 = jnp.float32

    asked = pl.pallas_call(
        ask_kernel,
        in_specs=[VMEM],
        out_specs=VMEM,
        out_shape=jax.ShapeDtypeStruct((devices, order), jnp.int32),
        compiler_params=pltpu.CompilerParams(vmem_limit_bytes=4 * MIB),
    )(tile_col[0].T)
    want = lax.all_to_all(asked[:, None], BOTH, 0, 0, tiled=True)[:, 0]

    lane = jnp.arange(order, dtype=jnp.int32)
    mine = jnp.where(lane < 2 * owned, lax.axis_index("row") * owned + lane % owned, -1)[None, :]

    chunks = 8
    small = jax.ShapeDtypeStruct((owned, order), f32)
    held, place, direction = pl.pallas_call(
        tile_kernel,
        in_specs=[pl.BlockSpec(memory_space=pltpu.HBM)] * 3 + [VMEM],
        out_specs=[pl.BlockSpec(memory_space=pltpu.HBM), VMEM, VMEM],
        out_shape=[
            pltpu.HBM((wanted, 2 * order, order), jnp.bfloat16),
            jax.ShapeDtypeStruct((wanted, owned, order), f32),
            small,
        ],
        scratch_shapes=[
            pltpu.VMEM((wanted, order, order), f32),
            pltpu.VMEM((wanted, 2 * order, order), jnp.bfloat16),
            pltpu.VMEM((slots, groups), jnp.int32),
            pltpu.VMEM((owned, order), f32),
            pltpu.SemaphoreType.DMA((chunks,)),
            pltpu.SemaphoreType.DMA((chunks,)),
            pltpu.SemaphoreType.DMA,
            pltpu.SemaphoreType.DMA,
        ],
        compiler_params=pltpu.CompilerParams(vmem_limit_bytes=16 * MIB),
    )(in_hbm(tiles.reshape(wanted, order, order)), in_hbm(tile_row[0].T), in_hbm(rhs), mine)

    pick, send = pl.pallas_call(
        start_kernel,
        in_specs=[VMEM] * 3,
        out_specs=[VMEM] * 2,
        out_shape=[
            jax.ShapeDtypeStruct((devices * slots, order), jnp.bfloat16),
            jax.ShapeDtypeStruct((devices * slots, order), f32),
        ],
        scratch_shapes=[pltpu.VMEM((devices * slots, order), f32)],
        cost_estimate=pl.CostEstimate(flops=10**10, transcendentals=0, bytes_accessed=4 * 10**7),
        compiler_params=pltpu.CompilerParams(vmem_limit_bytes=16 * MIB),
    )(want, mine, direction)

    pressure, residual = [], rhs
    for index, (keep, gain) in enumerate(steps()):
        first, last = index == 0, index == ITERS - 1
        got = lax.all_to_all(send.reshape(devices, slots, order), BOTH, 0, 0, tiled=True)
        outs = pl.pallas_call(
            functools.partial(step_kernel, keep, gain, first, last),
            in_specs=[VMEM] * (7 if first else 8),
            out_specs=[VMEM] * (2 if last else 4),
            out_shape=[small, small] if last else [small, small, small, jax.ShapeDtypeStruct((devices * slots, order), f32)],
            compiler_params=pltpu.CompilerParams(vmem_limit_bytes=16 * MIB),
        )(got.reshape(senders, wanted, order), held, place, pick, diag_vals, direction, residual, *pressure)
        pressure, residual = [outs[0]], outs[1]
        if not last:
            direction, send = outs[2:]
    return (pressure[0], residual)


def solution(mesh):
    return jax.shard_map(
        per_device,
        mesh=mesh,
        in_specs=(
            P(("row", "col"), None),
            P(("row", "col"), None),
            P(("row", "col"), None, None, None, None),
            P(("row", "col"), None, None),
            P(("row", "col"), None, None),
        ),
        out_specs=(P(("row", "col"), None), P(("row", "col"), None)),
        check_vma=False,
    )
```

```python
import functools

import jax
import jax.numpy as jnp
import numpy as np
from jax import lax
from jax.experimental import pallas as pl
from jax.experimental.pallas import tpu as pltpu
from jax.sharding import PartitionSpec as P

ITERS = 16

centre = 4.0
half_width = 3.96

BOTH = ("row", "col")
VMEM = pl.BlockSpec(memory_space=pltpu.VMEM)
MIB = 1 << 20
PLAIN = 1


def in_hbm(x):
    return pltpu.with_memory_space_constraint(x, pltpu.HBM)


def steps():
    sigma = np.float32(2.0 * (centre / half_width))
    rho = np.float32(1.0 / (centre / half_width))
    pairs = []
    for _ in range(ITERS):
        rho_new = np.float32(1.0) / (sigma - rho)
        pairs.append((float(rho_new * rho), float(np.float32(2.0) * rho_new / np.float32(half_width))))
        rho = rho_new
    return pairs


def to_send(pick, direction):
    high = direction.astype(jnp.bfloat16)
    low = (direction - high.astype(jnp.float32)).astype(jnp.bfloat16)
    parts = jnp.concatenate([high, low], axis=0)
    return jnp.dot(pick[:, : parts.shape[0]], parts, preferred_element_type=jnp.float32)


def ask_kernel(col_ref, ask_ref):
    slots, groups = col_ref.shape
    devices, lanes = ask_ref.shape
    wide = jnp.concatenate([col_ref[...], jnp.zeros((slots, lanes - groups), jnp.int32)], axis=1)
    wide = jnp.concatenate([wide, jnp.zeros((lanes - slots, lanes), jnp.int32)], axis=0)
    rows = wide.T[:groups]
    for first in range(0, devices, groups):
        ask_ref[first : first + groups] = rows


def tile_kernel(tile_hbm, row_hbm, rhs_hbm, mine_ref, held_hbm, plain_hbm, place_ref, direction_ref, tile_buf, held_buf, plain_buf, row_ref, rhs_ref, in_sem, out_sem, row_sem, rhs_sem):
    chunks = in_sem.shape[0]
    size = tile_hbm.shape[0] // chunks
    order = tile_hbm.shape[-1]
    fetches = [pltpu.make_async_copy(tile_hbm.at[pl.ds(c * size, size)], tile_buf.at[pl.ds(c * size, size)], in_sem.at[c]) for c in range(chunks)]
    stores = []
    for c in range(chunks):
        held_part = pl.ds(c * (size - PLAIN), size - PLAIN)
        plain_part = pl.ds(c * PLAIN, PLAIN)
        stores.append(pltpu.make_async_copy(held_buf.at[held_part], held_hbm.at[held_part], out_sem.at[c]))
        stores.append(pltpu.make_async_copy(plain_buf.at[plain_part], plain_hbm.at[plain_part], out_sem.at[chunks + c]))
    small = [pltpu.make_async_copy(row_hbm, row_ref, row_sem), pltpu.make_async_copy(rhs_hbm, rhs_ref, rhs_sem)]
    for fetch in small + fetches:
        fetch.start()
    for c in range(chunks):
        fetches[c].wait()
        for spot in range(size):
            flipped = tile_buf[c * size + spot].T
            if spot < PLAIN:
                plain_buf[c * PLAIN + spot] = flipped
            else:
                tile = c * (size - PLAIN) + spot - PLAIN
                high = flipped.astype(jnp.bfloat16)
                held_buf[tile, :order] = high
                held_buf[tile, order:] = (flipped - high.astype(jnp.float32)).astype(jnp.bfloat16)
        stores[2 * c].start()
        stores[2 * c + 1].start()
    for fetch in small:
        fetch.wait()
    direction_ref[...] = rhs_ref[...] * (1.0 / centre)
    slots, groups = row_ref.shape
    wanted, owned, spread = place_ref.shape
    source = lax.broadcasted_iota(jnp.int32, (groups, spread), 0)
    target = lax.broadcasted_iota(jnp.int32, (groups, spread), 1)
    targets = jnp.zeros((8, spread), jnp.float32)
    rows = row_ref[...].astype(jnp.float32)
    for slot in range(slots):
        expand = jnp.where(target == source * slots + slot, 1.0, 0.0).astype(jnp.bfloat16)
        line = jnp.broadcast_to(rows[slot : slot + 1], (8, groups)).astype(jnp.bfloat16)
        targets = targets + jnp.dot(line, expand, preferred_element_type=jnp.float32)
    targets = targets.astype(jnp.int32)
    block = lax.broadcasted_iota(jnp.int32, (8, spread), 0)
    for tile in range(wanted):
        line = jnp.broadcast_to(targets[:, tile : tile + 1], (8, spread))
        for first in range(0, owned, 8):
            place_ref[tile, first : first + 8] = jnp.where(block + first == line, 1.0, 0.0)
    for store in stores:
        store.wait()


def start_kernel(want_ref, mine_ref, direction_ref, pick_ref, send_ref, spread_ref):
    devices, lanes = want_ref.shape
    slots = spread_ref.shape[0] // devices
    mine = mine_ref[...]
    for slot in range(slots):
        asked = jnp.broadcast_to(want_ref[:, slot : slot + 1], (devices, lanes))
        spread_ref[pl.ds(slot, devices, stride=slots), :] = jnp.where(asked == mine, 1.0, 0.0)
    pick = spread_ref[...].astype(jnp.bfloat16)
    pick_ref[...] = pick
    send_ref[...] = to_send(pick, direction_ref[...])


def step_kernel(keep, gain, first, last, *refs):
    got_ref, held_ref, plain_ref, place_ref, pick_ref, diag_ref, direction_ref, residual_ref = refs[:8]
    out_refs = refs[8:] if first else refs[9:]
    senders, wanted, order = got_ref.shape
    vec = got_ref[0]
    for sender in range(1, senders):
        vec = vec + got_ref[sender]
    high = vec.astype(jnp.bfloat16).astype(jnp.float32)
    low = vec - high
    column = vec.T
    off = jnp.zeros(direction_ref.shape, jnp.float32)
    for block in range(wanted // 8):
        rows = slice(8 * block, 8 * block + 8)
        left = jnp.concatenate([high[rows], low[rows]], axis=0).astype(jnp.bfloat16)
        left = jnp.concatenate([left, left], axis=1)
        for slot in range(8):
            if slot < PLAIN:
                tile = 8 * block + slot
                row = jnp.zeros((8, order), jnp.float32)
                for part in range(0, order, 8):
                    row = row + plain_ref[PLAIN * block + slot, part : part + 8] * column[part : part + 8, tile : tile + 1]
                row = jnp.sum(row, axis=0, keepdims=True)
            else:
                out = jnp.dot(left, held_ref[(8 - PLAIN) * block + slot - PLAIN], preferred_element_type=jnp.float32)
                row = out[slot : slot + 1] + out[8 + slot : 9 + slot]
            off = off + place_ref[8 * block + slot] * row
    direction = direction_ref[...]
    residual = residual_ref[...] - (diag_ref[...] * direction - off)
    out_refs[0][...] = direction if first else refs[8][...] + direction
    out_refs[1][...] = residual
    if not last:
        direction = keep * direction + gain * residual
        out_refs[2][...] = direction
        out_refs[3][...] = to_send(pick_ref[...], direction)


def per_device(rhs, diag_vals, tiles, tile_row, tile_col):
    owned, order = rhs.shape
    _, groups, slots = tile_col.shape
    devices = lax.axis_size(BOTH)
    senders = devices // groups
    wanted = groups * slots
    f32 = jnp.float32

    asked = pl.pallas_call(
        ask_kernel,
        in_specs=[VMEM],
        out_specs=VMEM,
        out_shape=jax.ShapeDtypeStruct((devices, order), jnp.int32),
        compiler_params=pltpu.CompilerParams(vmem_limit_bytes=4 * MIB),
    )(tile_col[0].T)
    want = lax.all_to_all(asked[:, None], BOTH, 0, 0, tiled=True)[:, 0]

    lane = jnp.arange(order, dtype=jnp.int32)
    mine = jnp.where(lane < 2 * owned, lax.axis_index("row") * owned + lane % owned, -1)[None, :]

    chunks = 8
    small = jax.ShapeDtypeStruct((owned, order), f32)
    held_shape = ((8 - PLAIN) * chunks, 2 * order, order)
    plain_shape = (PLAIN * chunks, order, order)
    held, plain, place, direction = pl.pallas_call(
        tile_kernel,
        in_specs=[pl.BlockSpec(memory_space=pltpu.HBM)] * 3 + [VMEM],
        out_specs=[pl.BlockSpec(memory_space=pltpu.HBM)] * 2 + [VMEM, VMEM],
        out_shape=[
            pltpu.HBM(held_shape, jnp.bfloat16),
            pltpu.HBM(plain_shape, f32),
            jax.ShapeDtypeStruct((wanted, owned, order), f32),
            small,
        ],
        scratch_shapes=[
            pltpu.VMEM((wanted, order, order), f32),
            pltpu.VMEM(held_shape, jnp.bfloat16),
            pltpu.VMEM(plain_shape, f32),
            pltpu.VMEM((slots, groups), jnp.int32),
            pltpu.VMEM((owned, order), f32),
            pltpu.SemaphoreType.DMA((chunks,)),
            pltpu.SemaphoreType.DMA((2 * chunks,)),
            pltpu.SemaphoreType.DMA,
            pltpu.SemaphoreType.DMA,
        ],
        compiler_params=pltpu.CompilerParams(vmem_limit_bytes=16 * MIB),
    )(in_hbm(tiles.reshape(wanted, order, order)), in_hbm(tile_row[0].T), in_hbm(rhs), mine)

    pick, send = pl.pallas_call(
        start_kernel,
        in_specs=[VMEM] * 3,
        out_specs=[VMEM] * 2,
        out_shape=[
            jax.ShapeDtypeStruct((devices * slots, order), jnp.bfloat16),
            jax.ShapeDtypeStruct((devices * slots, order), f32),
        ],
        scratch_shapes=[pltpu.VMEM((devices * slots, order), f32)],
        cost_estimate=pl.CostEstimate(flops=10**10, transcendentals=0, bytes_accessed=4 * 10**7),
        compiler_params=pltpu.CompilerParams(vmem_limit_bytes=16 * MIB),
    )(want, mine, direction)

    pressure, residual = [], rhs
    for index, (keep, gain) in enumerate(steps()):
        first, last = index == 0, index == ITERS - 1
        got = lax.all_to_all(send.reshape(devices, slots, order), BOTH, 0, 0, tiled=True)
        outs = pl.pallas_call(
            functools.partial(step_kernel, keep, gain, first, last),
            in_specs=[VMEM] * (8 if first else 9),
            out_specs=[VMEM] * (2 if last else 4),
            out_shape=[small, small] if last else [small, small, small, jax.ShapeDtypeStruct((devices * slots, order), f32)],
            compiler_params=pltpu.CompilerParams(vmem_limit_bytes=16 * MIB),
        )(got.reshape(senders, wanted, order), held, plain, place, pick, diag_vals, direction, residual, *pressure)
        pressure, residual = [outs[0]], outs[1]
        if not last:
            direction, send = outs[2:]
    return (pressure[0], residual)


def solution(mesh):
    return jax.shard_map(
        per_device,
        mesh=mesh,
        in_specs=(
            P(("row", "col"), None),
            P(("row", "col"), None),
            P(("row", "col"), None, None, None, None),
            P(("row", "col"), None, None),
            P(("row", "col"), None, None),
        ),
        out_specs=(P(("row", "col"), None), P(("row", "col"), None)),
        check_vma=False,
    )
```

```python
import functools

import jax
import jax.numpy as jnp
import numpy as np
from jax import lax
from jax.experimental import pallas as pl
from jax.experimental.pallas import tpu as pltpu
from jax.sharding import PartitionSpec as P

ITERS = 16

centre = 4.0
half_width = 3.96

BOTH = ("row", "col")
VMEM = pl.BlockSpec(memory_space=pltpu.VMEM)
MIB = 1 << 20
PLAIN = 1


def in_hbm(x):
    return pltpu.with_memory_space_constraint(x, pltpu.HBM)


def steps():
    sigma = np.float32(2.0 * (centre / half_width))
    rho = np.float32(1.0 / (centre / half_width))
    pairs = []
    for _ in range(ITERS):
        rho_new = np.float32(1.0) / (sigma - rho)
        pairs.append((float(rho_new * rho), float(np.float32(2.0) * rho_new / np.float32(half_width))))
        rho = rho_new
    return pairs


def to_send(pick, direction):
    high = direction.astype(jnp.bfloat16)
    low = (direction - high.astype(jnp.float32)).astype(jnp.bfloat16)
    parts = jnp.concatenate([high, low], axis=0)
    return jnp.dot(pick[:, : parts.shape[0]], parts, preferred_element_type=jnp.float32)


def ask_kernel(col_ref, ask_ref):
    slots, groups = col_ref.shape
    devices, lanes = ask_ref.shape
    wide = jnp.concatenate([col_ref[...], jnp.zeros((slots, lanes - groups), jnp.int32)], axis=1)
    wide = jnp.concatenate([wide, jnp.zeros((lanes - slots, lanes), jnp.int32)], axis=0)
    rows = wide.T[:groups]
    for first in range(0, devices, groups):
        ask_ref[first : first + groups] = rows


def tile_kernel(tile_hbm, row_hbm, rhs_hbm, mine_ref, held_hbm, plain_hbm, place_ref, direction_ref, tile_buf, held_buf, plain_buf, row_ref, rhs_ref, in_sem, out_sem, row_sem, rhs_sem):
    chunks = in_sem.shape[0]
    size = tile_hbm.shape[0] // chunks
    order = tile_hbm.shape[-1]
    fetches = [pltpu.make_async_copy(tile_hbm.at[pl.ds(c * size, size)], tile_buf.at[pl.ds(c * size, size)], in_sem.at[c]) for c in range(chunks)]
    stores = []
    for c in range(chunks):
        held_part = pl.ds(c * (size - PLAIN), size - PLAIN)
        plain_part = pl.ds(c * PLAIN, PLAIN)
        stores.append(pltpu.make_async_copy(held_buf.at[held_part], held_hbm.at[held_part], out_sem.at[c]))
        stores.append(pltpu.make_async_copy(plain_buf.at[plain_part], plain_hbm.at[plain_part], out_sem.at[chunks + c]))
    small = [pltpu.make_async_copy(row_hbm, row_ref, row_sem), pltpu.make_async_copy(rhs_hbm, rhs_ref, rhs_sem)]
    for fetch in small + fetches:
        fetch.start()
    for c in range(chunks):
        fetches[c].wait()
        for spot in range(size):
            flipped = tile_buf[c * size + spot].T
            if spot < PLAIN:
                plain_buf[c * PLAIN + spot] = flipped
            else:
                tile = c * (size - PLAIN) + spot - PLAIN
                high = flipped.astype(jnp.bfloat16)
                held_buf[tile, :order] = high
                held_buf[tile, order:] = (flipped - high.astype(jnp.float32)).astype(jnp.bfloat16)
        stores[2 * c].start()
        stores[2 * c + 1].start()
    for fetch in small:
        fetch.wait()
    direction_ref[...] = rhs_ref[...] * (1.0 / centre)
    slots, groups = row_ref.shape
    wanted, owned, spread = place_ref.shape
    source = lax.broadcasted_iota(jnp.int32, (groups, spread), 0)
    target = lax.broadcasted_iota(jnp.int32, (groups, spread), 1)
    targets = jnp.zeros((8, spread), jnp.float32)
    rows = row_ref[...].astype(jnp.float32)
    for slot in range(slots):
        expand = jnp.where(target == source * slots + slot, 1.0, 0.0).astype(jnp.bfloat16)
        line = jnp.broadcast_to(rows[slot : slot + 1], (8, groups)).astype(jnp.bfloat16)
        targets = targets + jnp.dot(line, expand, preferred_element_type=jnp.float32)
    targets = targets.astype(jnp.int32)
    block = lax.broadcasted_iota(jnp.int32, (8, spread), 0)
    for tile in range(wanted):
        line = jnp.broadcast_to(targets[:, tile : tile + 1], (8, spread))
        for first in range(0, owned, 8):
            place_ref[tile, first : first + 8] = jnp.where(block + first == line, 1.0, 0.0)
    for store in stores:
        store.wait()


def start_kernel(want_ref, mine_ref, direction_ref, pick_ref, send_ref, spread_ref):
    devices, lanes = want_ref.shape
    slots = spread_ref.shape[0] // devices
    mine = mine_ref[...]
    for slot in range(slots):
        asked = jnp.broadcast_to(want_ref[:, slot : slot + 1], (devices, lanes))
        spread_ref[pl.ds(slot, devices, stride=slots), :] = jnp.where(asked == mine, 1.0, 0.0)
    pick = spread_ref[...].astype(jnp.bfloat16)
    pick_ref[...] = pick
    send_ref[...] = to_send(pick, direction_ref[...])


def step_kernel(keep, gain, last, *refs):
    got_ref, held_ref, plain_ref, place_ref, pick_ref, diag_ref, direction_ref, residual_ref = refs[:8]
    out_refs = refs[8:] if last else refs[9:]
    senders, wanted, order = got_ref.shape
    vec = got_ref[0]
    for sender in range(1, senders):
        vec = vec + got_ref[sender]
    high = vec.astype(jnp.bfloat16).astype(jnp.float32)
    low = vec - high
    column = vec.T
    off = jnp.zeros(direction_ref.shape, jnp.float32)
    for block in range(wanted // 8):
        rows = slice(8 * block, 8 * block + 8)
        left = jnp.concatenate([high[rows], low[rows]], axis=0).astype(jnp.bfloat16)
        left = jnp.concatenate([left, left], axis=1)
        for slot in range(8):
            if slot < PLAIN:
                tile = 8 * block + slot
                row = jnp.zeros((8, order), jnp.float32)
                for part in range(0, order, 8):
                    row = row + plain_ref[PLAIN * block + slot, part : part + 8] * column[part : part + 8, tile : tile + 1]
                row = jnp.sum(row, axis=0, keepdims=True)
            else:
                out = jnp.dot(left, held_ref[(8 - PLAIN) * block + slot - PLAIN], preferred_element_type=jnp.float32)
                row = out[slot : slot + 1] + out[8 + slot : 9 + slot]
            off = off + place_ref[8 * block + slot] * row
    direction = direction_ref[...]
    residual = residual_ref[...] - (diag_ref[...] * direction - off)
    out_refs[0][...] = residual
    if not last:
        direction = keep * direction + gain * residual
        out_refs[1][...] = direction
        out_refs[2][...] = to_send(pick_ref[...], direction)
        out_refs[3][...] = refs[8][...] + direction


def per_device(rhs, diag_vals, tiles, tile_row, tile_col):
    owned, order = rhs.shape
    _, groups, slots = tile_col.shape
    devices = lax.axis_size(BOTH)
    senders = devices // groups
    wanted = groups * slots
    f32 = jnp.float32

    asked = pl.pallas_call(
        ask_kernel,
        in_specs=[VMEM],
        out_specs=VMEM,
        out_shape=jax.ShapeDtypeStruct((devices, order), jnp.int32),
        compiler_params=pltpu.CompilerParams(vmem_limit_bytes=4 * MIB),
    )(tile_col[0].T)
    want = lax.all_to_all(asked[:, None], BOTH, 0, 0, tiled=True)[:, 0]

    lane = jnp.arange(order, dtype=jnp.int32)
    mine = jnp.where(lane < 2 * owned, lax.axis_index("row") * owned + lane % owned, -1)[None, :]

    chunks = 8
    small = jax.ShapeDtypeStruct((owned, order), f32)
    held_shape = ((8 - PLAIN) * chunks, 2 * order, order)
    plain_shape = (PLAIN * chunks, order, order)
    held, plain, place, direction = pl.pallas_call(
        tile_kernel,
        in_specs=[pl.BlockSpec(memory_space=pltpu.HBM)] * 3 + [VMEM],
        out_specs=[pl.BlockSpec(memory_space=pltpu.HBM)] * 2 + [VMEM, VMEM],
        out_shape=[
            pltpu.HBM(held_shape, jnp.bfloat16),
            pltpu.HBM(plain_shape, f32),
            jax.ShapeDtypeStruct((wanted, owned, order), f32),
            small,
        ],
        scratch_shapes=[
            pltpu.VMEM((wanted, order, order), f32),
            pltpu.VMEM(held_shape, jnp.bfloat16),
            pltpu.VMEM(plain_shape, f32),
            pltpu.VMEM((slots, groups), jnp.int32),
            pltpu.VMEM((owned, order), f32),
            pltpu.SemaphoreType.DMA((chunks,)),
            pltpu.SemaphoreType.DMA((2 * chunks,)),
            pltpu.SemaphoreType.DMA,
            pltpu.SemaphoreType.DMA,
        ],
        compiler_params=pltpu.CompilerParams(vmem_limit_bytes=16 * MIB),
    )(in_hbm(tiles.reshape(wanted, order, order)), in_hbm(tile_row[0].T), in_hbm(rhs), mine)

    pick, send = pl.pallas_call(
        start_kernel,
        in_specs=[VMEM] * 3,
        out_specs=[VMEM] * 2,
        out_shape=[
            jax.ShapeDtypeStruct((devices * slots, order), jnp.bfloat16),
            jax.ShapeDtypeStruct((devices * slots, order), f32),
        ],
        scratch_shapes=[pltpu.VMEM((devices * slots, order), f32)],
        cost_estimate=pl.CostEstimate(flops=10**10, transcendentals=0, bytes_accessed=4 * 10**7),
        compiler_params=pltpu.CompilerParams(vmem_limit_bytes=16 * MIB),
    )(want, mine, direction)

    pressure, residual = direction, rhs
    for index, (keep, gain) in enumerate(steps()):
        last = index == ITERS - 1
        got = lax.all_to_all(send.reshape(devices, slots, order), BOTH, 0, 0, tiled=True)
        outs = pl.pallas_call(
            functools.partial(step_kernel, keep, gain, last),
            in_specs=[VMEM] * (8 if last else 9),
            out_specs=[VMEM] * (1 if last else 4),
            out_shape=[small] if last else [small, small, jax.ShapeDtypeStruct((devices * slots, order), f32), small],
            compiler_params=pltpu.CompilerParams(vmem_limit_bytes=16 * MIB),
        )(got.reshape(senders, wanted, order), held, plain, place, pick, diag_vals, direction, residual, *([] if last else [pressure]))
        residual = outs[0]
        if not last:
            direction, send, pressure = outs[1:]
    return (pressure, residual)


def solution(mesh):
    return jax.shard_map(
        per_device,
        mesh=mesh,
        in_specs=(
            P(("row", "col"), None),
            P(("row", "col"), None),
            P(("row", "col"), None, None, None, None),
            P(("row", "col"), None, None),
            P(("row", "col"), None, None),
        ),
        out_specs=(P(("row", "col"), None), P(("row", "col"), None)),
        check_vma=False,
    )
```

```python
import functools

import jax
import jax.numpy as jnp
import numpy as np
from jax import lax
from jax.experimental import pallas as pl
from jax.experimental.pallas import tpu as pltpu
from jax.sharding import PartitionSpec as P

ITERS = 16

centre = 4.0
half_width = 3.96

BOTH = ("row", "col")
VMEM = pl.BlockSpec(memory_space=pltpu.VMEM)
MIB = 1 << 20
PLAIN = 1


def in_hbm(x):
    return pltpu.with_memory_space_constraint(x, pltpu.HBM)


def steps():
    sigma = np.float32(2.0 * (centre / half_width))
    rho = np.float32(1.0 / (centre / half_width))
    pairs = []
    for _ in range(ITERS):
        rho_new = np.float32(1.0) / (sigma - rho)
        pairs.append((float(rho_new * rho), float(np.float32(2.0) * rho_new / np.float32(half_width))))
        rho = rho_new
    return pairs


def to_send(pick, direction):
    high = direction.astype(jnp.bfloat16)
    low = (direction - high.astype(jnp.float32)).astype(jnp.bfloat16)
    parts = jnp.concatenate([high, low], axis=0)
    return jnp.dot(pick[:, : parts.shape[0]], parts, preferred_element_type=jnp.float32)


def ask_kernel(col_ref, ask_ref):
    slots, groups = col_ref.shape
    devices, lanes = ask_ref.shape
    wide = jnp.concatenate([col_ref[...], jnp.zeros((slots, lanes - groups), jnp.int32)], axis=1)
    wide = jnp.concatenate([wide, jnp.zeros((lanes - slots, lanes), jnp.int32)], axis=0)
    rows = wide.T[:groups]
    for first in range(0, devices, groups):
        ask_ref[first : first + groups] = rows


def tile_kernel(tile_hbm, row_hbm, rhs_hbm, mine_ref, held_hbm, plain_hbm, place_ref, direction_ref, tile_buf, held_buf, plain_buf, row_ref, rhs_ref, in_sem, out_sem, row_sem, rhs_sem):
    chunks = in_sem.shape[0]
    size = tile_hbm.shape[0] // chunks
    order = tile_hbm.shape[-1]
    fetches = [pltpu.make_async_copy(tile_hbm.at[pl.ds(c * size, size)], tile_buf.at[pl.ds(c * size, size)], in_sem.at[c]) for c in range(chunks)]
    stores = []
    for c in range(chunks):
        held_part = pl.ds(c * (size - PLAIN), size - PLAIN)
        plain_part = pl.ds(c * PLAIN, PLAIN)
        stores.append(pltpu.make_async_copy(held_buf.at[held_part], held_hbm.at[held_part], out_sem.at[c]))
        stores.append(pltpu.make_async_copy(plain_buf.at[plain_part], plain_hbm.at[plain_part], out_sem.at[chunks + c]))
    small = [pltpu.make_async_copy(row_hbm, row_ref, row_sem), pltpu.make_async_copy(rhs_hbm, rhs_ref, rhs_sem)]
    for fetch in small + fetches:
        fetch.start()
    for c in range(chunks):
        fetches[c].wait()
        for spot in range(size):
            flipped = tile_buf[c * size + spot].T
            if spot >= size - PLAIN:
                plain_buf[c * PLAIN + spot - (size - PLAIN)] = flipped
            else:
                tile = c * (size - PLAIN) + spot
                high = flipped.astype(jnp.bfloat16)
                held_buf[tile, :order] = high
                held_buf[tile, order:] = (flipped - high.astype(jnp.float32)).astype(jnp.bfloat16)
        stores[2 * c].start()
        stores[2 * c + 1].start()
    for fetch in small:
        fetch.wait()
    direction_ref[...] = rhs_ref[...] * (1.0 / centre)
    slots, groups = row_ref.shape
    wanted, owned, spread = place_ref.shape
    source = lax.broadcasted_iota(jnp.int32, (groups, spread), 0)
    target = lax.broadcasted_iota(jnp.int32, (groups, spread), 1)
    targets = jnp.zeros((8, spread), jnp.float32)
    rows = row_ref[...].astype(jnp.float32)
    for slot in range(slots):
        expand = jnp.where(target == source * slots + slot, 1.0, 0.0).astype(jnp.bfloat16)
        line = jnp.broadcast_to(rows[slot : slot + 1], (8, groups)).astype(jnp.bfloat16)
        targets = targets + jnp.dot(line, expand, preferred_element_type=jnp.float32)
    targets = targets.astype(jnp.int32)
    block = lax.broadcasted_iota(jnp.int32, (8, spread), 0)
    for tile in range(wanted):
        line = jnp.broadcast_to(targets[:, tile : tile + 1], (8, spread))
        for first in range(0, owned, 8):
            place_ref[tile, first : first + 8] = jnp.where(block + first == line, 1.0, 0.0)
    for store in stores:
        store.wait()


def start_kernel(want_ref, mine_ref, direction_ref, pick_ref, send_ref, spread_ref):
    devices, lanes = want_ref.shape
    slots = spread_ref.shape[0] // devices
    mine = mine_ref[...]
    for slot in range(slots):
        asked = jnp.broadcast_to(want_ref[:, slot : slot + 1], (devices, lanes))
        spread_ref[pl.ds(slot, devices, stride=slots), :] = jnp.where(asked == mine, 1.0, 0.0)
    pick = spread_ref[...].astype(jnp.bfloat16)
    pick_ref[...] = pick
    send_ref[...] = to_send(pick, direction_ref[...])


def step_kernel(keep, gain, first, last, *refs):
    got_ref, held_ref, plain_ref, place_ref, pick_ref, diag_ref, direction_ref, residual_ref = refs[:8]
    out_refs = refs[8:] if first else refs[9:]
    senders, wanted, order = got_ref.shape
    vec = got_ref[0]
    for sender in range(1, senders):
        vec = vec + got_ref[sender]
    high = vec.astype(jnp.bfloat16).astype(jnp.float32)
    low = vec - high
    column = vec.T
    off = jnp.zeros(direction_ref.shape, jnp.float32)
    for block in range(wanted // 8):
        rows = slice(8 * block, 8 * block + 8)
        left = jnp.concatenate([high[rows], low[rows]], axis=0).astype(jnp.bfloat16)
        left = jnp.concatenate([left, left], axis=1)
        for slot in range(8):
            if slot >= 8 - PLAIN:
                tile = 8 * block + slot
                row = jnp.zeros((8, order), jnp.float32)
                for part in range(0, order, 8):
                    row = row + plain_ref[PLAIN * block + slot - (8 - PLAIN), part : part + 8] * column[part : part + 8, tile : tile + 1]
                row = jnp.sum(row, axis=0, keepdims=True)
            else:
                out = jnp.dot(left, held_ref[(8 - PLAIN) * block + slot], preferred_element_type=jnp.float32)
                row = out[slot : slot + 1] + out[8 + slot : 9 + slot]
            off = off + place_ref[8 * block + slot] * row
    direction = direction_ref[...]
    residual = residual_ref[...] - (diag_ref[...] * direction - off)
    out_refs[0][...] = direction if first else refs[8][...] + direction
    out_refs[1][...] = residual
    if not last:
        direction = keep * direction + gain * residual
        out_refs[2][...] = direction
        out_refs[3][...] = to_send(pick_ref[...], direction)


def per_device(rhs, diag_vals, tiles, tile_row, tile_col):
    owned, order = rhs.shape
    _, groups, slots = tile_col.shape
    devices = lax.axis_size(BOTH)
    senders = devices // groups
    wanted = groups * slots
    f32 = jnp.float32

    asked = pl.pallas_call(
        ask_kernel,
        in_specs=[VMEM],
        out_specs=VMEM,
        out_shape=jax.ShapeDtypeStruct((devices, order), jnp.int32),
        compiler_params=pltpu.CompilerParams(vmem_limit_bytes=4 * MIB),
    )(tile_col[0].T)
    want = lax.all_to_all(asked[:, None], BOTH, 0, 0, tiled=True)[:, 0]

    lane = jnp.arange(order, dtype=jnp.int32)
    mine = jnp.where(lane < 2 * owned, lax.axis_index("row") * owned + lane % owned, -1)[None, :]

    chunks = 8
    small = jax.ShapeDtypeStruct((owned, order), f32)
    held_shape = ((8 - PLAIN) * chunks, 2 * order, order)
    plain_shape = (PLAIN * chunks, order, order)
    held, plain, place, direction = pl.pallas_call(
        tile_kernel,
        in_specs=[pl.BlockSpec(memory_space=pltpu.HBM)] * 3 + [VMEM],
        out_specs=[pl.BlockSpec(memory_space=pltpu.HBM)] * 2 + [VMEM, VMEM],
        out_shape=[
            pltpu.HBM(held_shape, jnp.bfloat16),
            pltpu.HBM(plain_shape, f32),
            jax.ShapeDtypeStruct((wanted, owned, order), f32),
            small,
        ],
        scratch_shapes=[
            pltpu.VMEM((wanted, order, order), f32),
            pltpu.VMEM(held_shape, jnp.bfloat16),
            pltpu.VMEM(plain_shape, f32),
            pltpu.VMEM((slots, groups), jnp.int32),
            pltpu.VMEM((owned, order), f32),
            pltpu.SemaphoreType.DMA((chunks,)),
            pltpu.SemaphoreType.DMA((2 * chunks,)),
            pltpu.SemaphoreType.DMA,
            pltpu.SemaphoreType.DMA,
        ],
        compiler_params=pltpu.CompilerParams(vmem_limit_bytes=16 * MIB),
    )(in_hbm(tiles.reshape(wanted, order, order)), in_hbm(tile_row[0].T), in_hbm(rhs), mine)

    pick, send = pl.pallas_call(
        start_kernel,
        in_specs=[VMEM] * 3,
        out_specs=[VMEM] * 2,
        out_shape=[
            jax.ShapeDtypeStruct((devices * slots, order), jnp.bfloat16),
            jax.ShapeDtypeStruct((devices * slots, order), f32),
        ],
        scratch_shapes=[pltpu.VMEM((devices * slots, order), f32)],
        cost_estimate=pl.CostEstimate(flops=10**10, transcendentals=0, bytes_accessed=4 * 10**7),
        compiler_params=pltpu.CompilerParams(vmem_limit_bytes=16 * MIB),
    )(want, mine, direction)

    pressure, residual = [], rhs
    for index, (keep, gain) in enumerate(steps()):
        first, last = index == 0, index == ITERS - 1
        got = lax.all_to_all(send.reshape(devices, slots, order), BOTH, 0, 0, tiled=True)
        outs = pl.pallas_call(
            functools.partial(step_kernel, keep, gain, first, last),
            in_specs=[VMEM] * (8 if first else 9),
            out_specs=[VMEM] * (2 if last else 4),
            out_shape=[small, small] if last else [small, small, small, jax.ShapeDtypeStruct((devices * slots, order), f32)],
            compiler_params=pltpu.CompilerParams(vmem_limit_bytes=16 * MIB),
        )(got.reshape(senders, wanted, order), held, plain, place, pick, diag_vals, direction, residual, *pressure)
        pressure, residual = [outs[0]], outs[1]
        if not last:
            direction, send = outs[2:]
    return (pressure[0], residual)


def solution(mesh):
    return jax.shard_map(
        per_device,
        mesh=mesh,
        in_specs=(
            P(("row", "col"), None),
            P(("row", "col"), None),
            P(("row", "col"), None, None, None, None),
            P(("row", "col"), None, None),
            P(("row", "col"), None, None),
        ),
        out_specs=(P(("row", "col"), None), P(("row", "col"), None)),
        check_vma=False,
    )
```
